256 devices in a mesh: row: 8 (over x, core), col: 16 (over z, y_hi), layer: 2 (over y_lo).
Axes of the slice: x: 4, y: 4 (y_hi: 2, y_lo: 2; y = y_hi * 2 + y_lo), z: 8, core: 2. Of those that a mesh axis runs over, the one named last changes fastest.
Arguments:
- interface_panel: float32 [2048, 1024], P('col', 'row'), may hold values from -6 to 6
- coupling: float32 [2, 2, 2048, 2048], P('layer', None, 'row', 'col'), may hold values from -0.0625 to 0.0625
- solved_coupling: float32 [8192, 1024], P(('layer', 'col'), 'row'), may hold values from -6 to 6
Outputs:
- schur_panel: float32 [2048, 1024], P('col', 'row')
The draws below stay inside these ranges and needn't reach their ends.
All inputs are finite; a program needn't handle non-finite values.
Results may differ from the reference program's by a relative error of at most 0.00007.
Values sent between devices are 32-bit elements; how exact they have to be, the bound alone decides.
A program may use at most 64 MiB of HBM per device.

```python
import jax
import jax.numpy as jnp
from jax import lax

P_SIZE = 1024
KB = 256
SLOTS = 2
K = 8192
M = 2048
N_ROW = 8
N_LAYER = 2


def level_of(stream_key, extent, shards, low, largest):
    def one(axis_at, blocks):
        draws = jax.random.uniform(jax.random.fold_in(jax.random.fold_in(stream_key, 6), axis_at), (blocks,), jnp.float32, low / len(shards), largest / len(shards))
        return jnp.repeat(jnp.exp(draws), extent[axis_at] // blocks).reshape((-1,) + (1,) * (len(extent) - axis_at - 1))

    factor_of = one(*shards[0])
    for cut in shards[1:]:
        factor_of = factor_of * one(*cut)
    return factor_of


def scatter_about(key, shape, scale, bound, pieces=(), kind=jnp.bfloat16):
    level = level_of(key, shape, pieces, -0.22, 0.18) if pieces else 1.0
    result = jax.random.normal(key, shape, jnp.float32) * scale * level
    return jnp.minimum(jnp.maximum(result, -bound), bound).astype(kind)


def setup_inputs(seed: int = 0) -> dict:
    key_of = jax.random.split(jax.random.key(seed), 4)
    interface_panel = scatter_about(key_of[0], (M, P_SIZE), 1.0, 6.0, ((0, 16), (1, 8)), jnp.float32)
    coupling = scatter_about(key_of[1], (N_LAYER, SLOTS, N_ROW * KB, M), K ** -0.5, 0.0625, ((0, 2), (2, 8), (3, 16)), jnp.float32)
    solved_coupling = scatter_about(key_of[2], (K, P_SIZE), 1.0, 6.0, ((0, 32), (1, 8)), jnp.float32)
    return {"interface_panel": interface_panel, "coupling": coupling, "solved_coupling": solved_coupling}


def reference(interface_panel, coupling, solved_coupling):
    depth = coupling.shape[0] * coupling.shape[1] * coupling.shape[2]
    coupling_matrix = coupling.reshape(depth, coupling.shape[3])
    product = jnp.dot(coupling_matrix.T, solved_coupling, preferred_element_type=jnp.float32, precision=lax.Precision.HIGHEST)
    return interface_panel - product
```

```python
import jax
import jax.numpy as jnp
from jax import lax
from jax.sharding import PartitionSpec as P


def shards(interface_panel, coupling, solved_coupling):
    blocks = coupling[0]
    depth = blocks.shape[0] * blocks.shape[1] * lax.axis_size("row")
    gathered_b = lax.all_gather(blocks, "row", axis=1, tiled=True).reshape(depth, blocks.shape[2])
    gathered_y = lax.all_gather(solved_coupling, "col", axis=0, tiled=True)
    partial = lax.dot_general(
        gathered_b,
        gathered_y,
        (((0,), (0,)), ((), ())),
        precision=lax.Precision.HIGHEST,
        preferred_element_type=jnp.float32,
    )
    other = lax.ppermute(partial, "layer", [(0, 1), (1, 0)])
    return interface_panel - (partial + other)


def solution(mesh):
    return jax.shard_map(
        shards,
        mesh=mesh,
        in_specs=(P("col", "row"), P("layer", None, "row", "col"), P(("layer", "col"), "row")),
        out_specs=P("col", "row"),
        check_vma=False,
    )
```

```python
import jax
import jax.numpy as jnp
from jax import lax
from jax.experimental import pallas as pl
from jax.experimental.pallas import tpu as pltpu
from jax.sharding import PartitionSpec as P

MESH = pl.DeviceIdType.MESH


def multiply(block, solved):
    return lax.dot_general(
        block,
        solved,
        (((0,), (0,)), ((), ())),
        precision=lax.Precision.HIGHEST,
        preferred_element_type=jnp.float32,
    )


def kernel(a_ref, b_ref, y_ref, o_ref, b_all, y_all, mine, theirs,
           b_send, b_recv, y_send, y_recv, p_send, p_recv):
    n_row = lax.axis_size("row")
    n_col = lax.axis_size("col")
    r = lax.axis_index("row")
    c = lax.axis_index("col")
    l = lax.axis_index("layer")
    partner = 1 - l

    def row_peer(d):
        return ((r + d) % n_row, c, l)

    def col_peer(d):
        return (r, (c + d) % n_col, l)

    barrier = pltpu.get_barrier_semaphore()
    for d in range(1, n_row):
        pl.semaphore_signal(barrier, 1, device_id=row_peer(d), device_id_type=MESH)
    for d in range(1, n_col):
        pl.semaphore_signal(barrier, 1, device_id=col_peer(d), device_id_type=MESH)
    pl.semaphore_signal(barrier, 1, device_id=(r, c, partner), device_id_type=MESH)
    pl.semaphore_wait(barrier, (n_row - 1) + (n_col - 1) + 1)

    sends = []
    for d in range(1, n_row):
        copy = pltpu.make_async_remote_copy(
            b_ref.at[0], b_all.at[r], b_send.at[d], b_recv.at[r],
            device_id=row_peer(d), device_id_type=MESH)
        copy.start()
        sends.append(copy)
    for d in range(1, n_col):
        copy = pltpu.make_async_remote_copy(
            y_ref, y_all.at[c], y_send.at[d], y_recv.at[c],
            device_id=col_peer(d), device_id_type=MESH)
        copy.start()
        sends.append(copy)

    b_all[r] = b_ref[0]
    y_all[c] = y_ref[...]

    for d in range(1, n_row):
        source = (r + n_row - d) % n_row
        pltpu.make_async_remote_copy(
            b_ref.at[0], b_all.at[source], b_send.at[d], b_recv.at[source],
            device_id=row_peer(d), device_id_type=MESH).wait_recv()

    total = jnp.zeros(mine.shape, jnp.float32)
    for d in range(n_col):
        source = (c + n_col - d) % n_col
        if d > 0:
            pltpu.make_async_remote_copy(
                y_ref, y_all.at[source], y_send.at[d], y_recv.at[source],
                device_id=col_peer(d), device_id_type=MESH).wait_recv()
        block = b_all[source % n_row, source // n_row]
        total = total + multiply(block, y_all[source])
    mine[...] = total

    swap = pltpu.make_async_remote_copy(
        mine, theirs, p_send.at[0], p_recv.at[0],
        device_id=(r, c, partner), device_id_type=MESH)
    swap.start()
    swap.wait()
    o_ref[...] = a_ref[...] - (mine[...] + theirs[...])
    for copy in sends:
        copy.wait_send()


def shards(interface_panel, coupling, solved_coupling):
    n_row = lax.axis_size("row")
    n_col = lax.axis_size("col")
    _, slots, depth, width = coupling.shape
    vmem = pl.BlockSpec(memory_space=pltpu.VMEM)
    rows, cols = interface_panel.shape
    return pl.pallas_call(
        kernel,
        out_shape=jax.ShapeDtypeStruct((rows, cols), jnp.float32),
        in_specs=[vmem, vmem, vmem],
        out_specs=vmem,
        scratch_shapes=[
            pltpu.VMEM((n_row, slots, depth, width), jnp.float32),
            pltpu.VMEM((n_col,) + solved_coupling.shape, jnp.float32),
            pltpu.VMEM((rows, cols), jnp.float32),
            pltpu.VMEM((rows, cols), jnp.float32),
            pltpu.SemaphoreType.DMA((n_row,)),
            pltpu.SemaphoreType.DMA((n_row,)),
            pltpu.SemaphoreType.DMA((n_col,)),
            pltpu.SemaphoreType.DMA((n_col,)),
            pltpu.SemaphoreType.DMA((1,)),
            pltpu.SemaphoreType.DMA((1,)),
        ],
        compiler_params=pltpu.CompilerParams(collective_id=0, has_side_effects=True),
    )(interface_panel, coupling, solved_coupling)


def solution(mesh):
    return jax.shard_map(
        shards,
        mesh=mesh,
        in_specs=(P("col", "row"), P("layer", None, "row", "col"), P(("layer", "col"), "row")),
        out_specs=P("col", "row"),
        check_vma=False,
    )
```

```python
import jax
import jax.numpy as jnp
from jax import lax
from jax.experimental import pallas as pl
from jax.experimental.pallas import tpu as pltpu
from jax.sharding import PartitionSpec as P

MESH = pl.DeviceIdType.MESH


def multiply(block, solved):
    return lax.dot_general(
        block,
        solved,
        (((0,), (0,)), ((), ())),
        precision=lax.Precision.HIGHEST,
        preferred_element_type=jnp.float32,
    )


def kernel(a_ref, b_ref, y_ref, o_ref, b_all, y_all, mine, theirs,
           b_send, b_recv, y_send, y_recv, p_send, p_recv):
    n_row = lax.axis_size("row")
    n_col = lax.axis_size("col")
    n_chip = n_row // 2
    n_z = n_col // 2
    r = lax.axis_index("row")
    c = lax.axis_index("col")
    l = lax.axis_index("layer")
    chip, core = r // 2, r % 2
    z, half = c // 2, c % 2
    other = 1 - half

    def row_dev(row):
        return (row, c, l)

    def col_dev(col):
        return (r, col, l)

    def col_of(zz, h):
        return ((zz + n_z) % n_z) * 2 + h

    cw = col_of(z + 1, half)
    ccw = col_of(z - 1, half)
    partner_col = col_of(z, other)
    on_chip = chip * 2 + (1 - core)

    def far_row(d):
        return ((chip + d) % n_chip) * 2 + core

    barrier = pltpu.get_barrier_semaphore()
    peers = [row_dev(far_row(d)) for d in range(1, n_chip)]
    peers += [row_dev(on_chip), col_dev(partner_col), col_dev(cw), col_dev(ccw), (r, c, 1 - l)]
    for peer in peers:
        pl.semaphore_signal(barrier, 1, device_id=peer, device_id_type=MESH)
    pl.semaphore_wait(barrier, len(peers))

    sends = []

    def send(src, dst, sems, recv_sems, slot, device):
        copy = pltpu.make_async_remote_copy(
            src, dst.at[slot], sems.at[len(sends)], recv_sems.at[slot],
            device_id=device, device_id_type=MESH)
        copy.start()
        sends.append(copy)

    def arrival(src, dst, recv_sems, slot):
        pltpu.make_async_remote_copy(
            src, dst.at[slot], recv_sems.at[slot], recv_sems.at[slot],
            device_id=(r, c, 1 - l), device_id_type=MESH).wait_recv()

    for d in range(1, n_chip):
        send(b_ref.at[0], b_all, b_send, b_recv, r, row_dev(far_row(d)))
    send(b_ref.at[0], b_all, b_send, b_recv, r, row_dev(on_chip))
    b_sends = len(sends)

    y_base = len(sends)

    def y_send_slot(src, slot, col):
        copy = pltpu.make_async_remote_copy(
            src, y_all.at[slot], y_send.at[len(sends) - y_base], y_recv.at[slot],
            device_id=col_dev(col), device_id_type=MESH)
        copy.start()
        sends.append(copy)

    def y_arrival(slot):
        arrival(y_ref, y_all, y_recv, slot)

    own_cw, own_ccw = n_z // 2, (n_z - 1) // 2
    far_cw, far_ccw = (n_z - 1) // 2, n_z // 2

    y_send_slot(y_ref, c, partner_col)
    if own_cw >= 1:
        y_send_slot(y_ref, c, cw)
    if own_ccw >= 1:
        y_send_slot(y_ref, c, ccw)
    b_all[r] = b_ref[0]
    y_all[c] = y_ref[...]
    y_arrival(partner_col)
    if far_cw >= 1:
        y_send_slot(y_all.at[partner_col], partner_col, cw)
    if far_ccw >= 1:
        y_send_slot(y_all.at[partner_col], partner_col, ccw)
    for t in range(2, n_z // 2 + 1):
        if t <= own_cw:
            slot = col_of(z - (t - 1), half)
            y_arrival(slot)
            y_send_slot(y_all.at[slot], slot, cw)
        if t <= own_ccw:
            slot = col_of(z + (t - 1), half)
            y_arrival(slot)
            y_send_slot(y_all.at[slot], slot, ccw)
        if t <= far_cw:
            slot = col_of(z - (t - 1), other)
            y_arrival(slot)
            y_send_slot(y_all.at[slot], slot, cw)
        if t <= far_ccw:
            slot = col_of(z + (t - 1), other)
            y_arrival(slot)
            y_send_slot(y_all.at[slot], slot, ccw)
    if own_cw >= 1:
        y_arrival(col_of(z - own_cw, half))
    if own_ccw >= 1:
        y_arrival(col_of(z + own_ccw, half))
    if far_cw >= 1:
        y_arrival(col_of(z - far_cw, other))
    if far_ccw >= 1:
        y_arrival(col_of(z + far_ccw, other))

    relay_base = len(sends)
    for d in range(1, n_chip):
        slot = far_row(d)
        arrival(b_ref.at[0], b_all, b_recv, slot)
        copy = pltpu.make_async_remote_copy(
            b_all.at[slot], b_all.at[slot], b_send.at[b_sends + len(sends) - relay_base],
            b_recv.at[slot], device_id=row_dev(on_chip), device_id_type=MESH)
        copy.start()
        sends.append(copy)
    arrival(b_ref.at[0], b_all, b_recv, on_chip)
    for d in range(1, n_chip):
        arrival(b_ref.at[0], b_all, b_recv, ((chip + d) % n_chip) * 2 + (1 - core))

    total = jnp.zeros(mine.shape, jnp.float32)
    for jj in range(n_col):
        total = total + multiply(b_all[jj % n_row, jj // n_row], y_all[jj])
    mine[...] = total

    swap = pltpu.make_async_remote_copy(
        mine, theirs, p_send.at[0], p_recv.at[0],
        device_id=(r, c, 1 - l), device_id_type=MESH)
    swap.start()
    swap.wait()
    o_ref[...] = a_ref[...] - (mine[...] + theirs[...])
    for copy in sends:
        copy.wait_send()


def shards(interface_panel, coupling, solved_coupling):
    n_row = lax.axis_size("row")
    n_col = lax.axis_size("col")
    _, slots, depth, width = coupling.shape
    vmem = pl.BlockSpec(memory_space=pltpu.VMEM)
    rows, cols = interface_panel.shape
    return pl.pallas_call(
        kernel,
        out_shape=jax.ShapeDtypeStruct((rows, cols), jnp.float32),
        in_specs=[vmem, vmem, vmem],
        out_specs=vmem,
        scratch_shapes=[
            pltpu.VMEM((n_row, slots, depth, width), jnp.float32),
            pltpu.VMEM((n_col,) + solved_coupling.shape, jnp.float32),
            pltpu.VMEM((rows, cols), jnp.float32),
            pltpu.VMEM((rows, cols), jnp.float32),
            pltpu.SemaphoreType.DMA((n_row,)),
            pltpu.SemaphoreType.DMA((n_row,)),
            pltpu.SemaphoreType.DMA((n_col,)),
            pltpu.SemaphoreType.DMA((n_col,)),
            pltpu.SemaphoreType.DMA((1,)),
            pltpu.SemaphoreType.DMA((1,)),
        ],
        compiler_params=pltpu.CompilerParams(collective_id=0, has_side_effects=True),
    )(interface_panel, coupling, solved_coupling)


def solution(mesh):
    return jax.shard_map(
        shards,
        mesh=mesh,
        in_specs=(P("col", "row"), P("layer", None, "row", "col"), P(("layer", "col"), "row")),
        out_specs=P("col", "row"),
        check_vma=False,
    )
```

```python
import jax
import jax.numpy as jnp
from jax import lax
from jax.experimental import pallas as pl
from jax.experimental.pallas import tpu as pltpu
from jax.sharding import PartitionSpec as P

MESH = pl.DeviceIdType.MESH


def multiply(block, solved):
    return lax.dot_general(
        block,
        solved,
        (((0,), (0,)), ((), ())),
        precision=lax.Precision.HIGHEST,
        preferred_element_type=jnp.float32,
    )


def kernel(a_ref, b_ref, y_ref, o_ref, b_all, y_all, own_part, far_part, got_far, summed, got_sum,
           b_send, b_recv, y_send, y_recv, p_send, p_recv):
    n_row = lax.axis_size("row")
    n_col = lax.axis_size("col")
    n_chip = n_row // 2
    n_z = n_col // 2
    slots = b_ref.shape[1]
    r = lax.axis_index("row")
    c = lax.axis_index("col")
    l = lax.axis_index("layer")
    chip, core = r // 2, r % 2
    z, half = c // 2, c % 2
    keeper = core == half

    def col_of(zz, h):
        return ((zz + n_z) % n_z) * 2 + h

    cw = col_of(z + 1, half)
    ccw = col_of(z - 1, half)
    partner_col = col_of(z, 1 - half)
    on_chip = chip * 2 + (1 - core)

    def far_row(d):
        return ((chip + d) % n_chip) * 2 + core

    cross = (on_chip, partner_col, l)
    diagonal = (r, partner_col, 1 - l)
    layer_peer = (r, c, 1 - l)

    barrier = pltpu.get_barrier_semaphore()
    peers = [(far_row(d), c, l) for d in range(1, n_chip)]
    peers += [(on_chip, c, l), cross, (r, cw, l), (r, ccw, l), diagonal, layer_peer]
    for peer in peers:
        pl.semaphore_signal(barrier, 1, device_id=peer, device_id_type=MESH)
    pl.semaphore_wait(barrier, len(peers))

    def arrival(src, dst, recv_sems, slot):
        pltpu.make_async_remote_copy(
            src, dst.at[slot], recv_sems.at[slot], recv_sems.at[slot],
            device_id=layer_peer, device_id_type=MESH).wait_recv()

    local_fill = pltpu.make_async_copy(b_ref.at[0], b_all.at[r], b_recv.at[r])
    cross_fill = pltpu.make_async_remote_copy(
        b_ref.at[0], b_all.at[on_chip], b_send.at[0], b_recv.at[on_chip],
        device_id=cross, device_id_type=MESH)

    @pl.when(keeper)
    def _():
        local_fill.start()

    @pl.when(jnp.logical_not(keeper))
    def _():
        cross_fill.start()

    sends = []

    def y_send_slot(src, slot, col):
        copy = pltpu.make_async_remote_copy(
            src, y_all.at[slot], y_send.at[len(sends)], y_recv.at[slot],
            device_id=(r, col, l), device_id_type=MESH)
        copy.start()
        sends.append(copy)

    def y_arrival(slot):
        arrival(y_ref, y_all, y_recv, slot)

    own_cw, own_ccw = n_z // 2, (n_z - 1) // 2
    if own_cw >= 1:
        y_send_slot(y_ref, c, cw)
    if own_ccw >= 1:
        y_send_slot(y_ref, c, ccw)
    y_all[c] = y_ref[...]

    @pl.when(keeper)
    def _():
        local_fill.wait()

    @pl.when(jnp.logical_not(keeper))
    def _():
        arrival(b_ref.at[0], b_all, b_recv, r)

    b_sends = []

    def b_send_slot(slot, row):
        copy = pltpu.make_async_remote_copy(
            b_all.at[slot], b_all.at[slot], b_send.at[1 + len(b_sends)], b_recv.at[slot],
            device_id=(row, c, l), device_id_type=MESH)
        copy.start()
        b_sends.append(copy)

    for d in range(1, n_chip):
        b_send_slot(r, far_row(d))
    b_send_slot(r, on_chip)

    for t in range(2, n_z // 2 + 1):
        if t <= own_cw:
            slot = col_of(z - (t - 1), half)
            y_arrival(slot)
            y_send_slot(y_all.at[slot], slot, cw)
        if t <= own_ccw:
            slot = col_of(z + (t - 1), half)
            y_arrival(slot)
            y_send_slot(y_all.at[slot], slot, ccw)

    for d in range(1, n_chip):
        slot = far_row(d)
        arrival(b_ref.at[0], b_all, b_recv, slot)
        b_send_slot(slot, on_chip)

    if own_cw >= 1:
        y_arrival(col_of(z - own_cw, half))
    if own_ccw >= 1:
        y_arrival(col_of(z + own_ccw, half))
    arrival(b_ref.at[0], b_all, b_recv, on_chip)
    for d in range(1, n_chip):
        arrival(b_ref.at[0], b_all, b_recv, ((chip + d) % n_chip) * 2 + (1 - core))

    own = jnp.zeros(own_part.shape, jnp.float32)
    far = jnp.zeros(far_part.shape, jnp.float32)
    for s in range(slots):
        for x in range(n_chip):
            jj = s * n_row + 2 * x + half
            solved = y_all[jj]
            own = own + multiply(b_all[2 * x + half, s], solved)
            far = far + multiply(b_all[2 * x + 1 - half, s], solved)
    own_part[...] = own
    far_part[...] = far

    first = pltpu.make_async_remote_copy(
        far_part, got_far, p_send.at[0], p_recv.at[0],
        device_id=diagonal, device_id_type=MESH)
    first.start()
    first.wait()
    summed[...] = own_part[...] + got_far[...]
    second = pltpu.make_async_remote_copy(
        summed, got_sum, p_send.at[1], p_recv.at[1],
        device_id=layer_peer, device_id_type=MESH)
    second.start()
    second.wait()
    o_ref[...] = a_ref[...] - (summed[...] + got_sum[...])

    for copy in sends + b_sends:
        copy.wait_send()

    @pl.when(jnp.logical_not(keeper))
    def _():
        cross_fill.wait_send()


def shards(interface_panel, coupling, solved_coupling):
    n_row = lax.axis_size("row")
    n_col = lax.axis_size("col")
    _, slots, depth, width = coupling.shape
    vmem = pl.BlockSpec(memory_space=pltpu.VMEM)
    rows, cols = interface_panel.shape
    part = pltpu.VMEM((rows, cols), jnp.float32)
    return pl.pallas_call(
        kernel,
        out_shape=jax.ShapeDtypeStruct((rows, cols), jnp.float32),
        in_specs=[vmem, vmem, vmem],
        out_specs=vmem,
        scratch_shapes=[
            pltpu.VMEM((n_row, slots, depth, width), jnp.float32),
            pltpu.VMEM((n_col,) + solved_coupling.shape, jnp.float32),
            part, part, part, part, part,
            pltpu.SemaphoreType.DMA((n_row + 1,)),
            pltpu.SemaphoreType.DMA((n_row,)),
            pltpu.SemaphoreType.DMA((n_col,)),
            pltpu.SemaphoreType.DMA((n_col,)),
            pltpu.SemaphoreType.DMA((2,)),
            pltpu.SemaphoreType.DMA((2,)),
        ],
        compiler_params=pltpu.CompilerParams(collective_id=0, has_side_effects=True),
    )(interface_panel, coupling, solved_coupling)


def solution(mesh):
    return jax.shard_map(
        shards,
        mesh=mesh,
        in_specs=(P("col", "row"), P("layer", None, "row", "col"), P(("layer", "col"), "row")),
        out_specs=P("col", "row"),
        check_vma=False,
    )
```

```python
import jax
import jax.numpy as jnp
from jax import lax
from jax.experimental import pallas as pl
from jax.experimental.pallas import tpu as pltpu
from jax.sharding import PartitionSpec as P

MESH = pl.DeviceIdType.MESH


def multiply(block, solved):
    return lax.dot_general(
        block,
        solved,
        (((0,), (0,)), ((), ())),
        precision=lax.Precision.HIGHEST,
        preferred_element_type=jnp.float32,
    )


def kernel(a_ref, b_ref, y_ref, o_ref, b_all, y_all, own_part, far_part, got_diag, got_plane, got_layer,
           b_send, b_recv, y_send, y_recv, p_send, p_recv):
    n_row = lax.axis_size("row")
    n_col = lax.axis_size("col")
    n_chip = n_row // 2
    n_z = n_col // 2
    slots = b_ref.shape[1]
    r = lax.axis_index("row")
    c = lax.axis_index("col")
    l = lax.axis_index("layer")
    chip, core = r // 2, r % 2
    z, half = c // 2, c % 2
    keeper = core == half

    def col_of(zz, h):
        return ((zz + n_z) % n_z) * 2 + h

    cw = col_of(z + 1, half)
    ccw = col_of(z - 1, half)
    partner_col = col_of(z, 1 - half)
    on_chip = chip * 2 + (1 - core)

    def far_row(d):
        return ((chip + d) % n_chip) * 2 + core

    cross = (on_chip, partner_col, l)
    diagonal = (r, partner_col, 1 - l)
    plane_peer = (r, partner_col, l)
    layer_peer = (r, c, 1 - l)

    barrier = pltpu.get_barrier_semaphore()
    peers = [(far_row(d), c, l) for d in range(1, n_chip)]
    peers += [(on_chip, c, l), cross, (r, cw, l), (r, ccw, l), diagonal, plane_peer, layer_peer]
    for peer in peers:
        pl.semaphore_signal(barrier, 1, device_id=peer, device_id_type=MESH)
    pl.semaphore_wait(barrier, len(peers))

    def arrival(src, dst, recv_sems, slot):
        pltpu.make_async_remote_copy(
            src, dst.at[slot], recv_sems.at[slot], recv_sems.at[slot],
            device_id=layer_peer, device_id_type=MESH).wait_recv()

    local_fill = pltpu.make_async_copy(b_ref.at[0], b_all.at[r], b_recv.at[r])
    cross_fill = pltpu.make_async_remote_copy(
        b_ref.at[0], b_all.at[on_chip], b_send.at[0], b_recv.at[on_chip],
        device_id=cross, device_id_type=MESH)

    @pl.when(keeper)
    def _():
        local_fill.start()

    @pl.when(jnp.logical_not(keeper))
    def _():
        cross_fill.start()

    sends = []

    def y_send_slot(src, slot, col):
        copy = pltpu.make_async_remote_copy(
            src, y_all.at[slot], y_send.at[len(sends)], y_recv.at[slot],
            device_id=(r, col, l), device_id_type=MESH)
        copy.start()
        sends.append(copy)

    def y_arrival(slot):
        arrival(y_ref, y_all, y_recv, slot)

    own_cw, own_ccw = n_z // 2, (n_z - 1) // 2
    if own_cw >= 1:
        y_send_slot(y_ref, c, cw)
    if own_ccw >= 1:
        y_send_slot(y_ref, c, ccw)
    y_all[c] = y_ref[...]

    @pl.when(keeper)
    def _():
        local_fill.wait()

    @pl.when(jnp.logical_not(keeper))
    def _():
        arrival(b_ref.at[0], b_all, b_recv, r)

    b_sends = []

    def b_send_slot(slot, row):
        copy = pltpu.make_async_remote_copy(
            b_all.at[slot], b_all.at[slot], b_send.at[1 + len(b_sends)], b_recv.at[slot],
            device_id=(row, c, l), device_id_type=MESH)
        copy.start()
        b_sends.append(copy)

    for d in range(1, n_chip):
        b_send_slot(r, far_row(d))
    b_send_slot(r, on_chip)

    for t in range(2, n_z // 2 + 1):
        if t <= own_cw:
            slot = col_of(z - (t - 1), half)
            y_arrival(slot)
            y_send_slot(y_all.at[slot], slot, cw)
        if t <= own_ccw:
            slot = col_of(z + (t - 1), half)
            y_arrival(slot)
            y_send_slot(y_all.at[slot], slot, ccw)

    for d in range(1, n_chip):
        slot = far_row(d)
        arrival(b_ref.at[0], b_all, b_recv, slot)
        b_send_slot(slot, on_chip)

    if own_cw >= 1:
        y_arrival(col_of(z - own_cw, half))
    if own_ccw >= 1:
        y_arrival(col_of(z + own_ccw, half))
    arrival(b_ref.at[0], b_all, b_recv, on_chip)
    for d in range(1, n_chip):
        arrival(b_ref.at[0], b_all, b_recv, ((chip + d) % n_chip) * 2 + (1 - core))

    far = jnp.zeros(far_part.shape, jnp.float32)
    for s in range(slots):
        for x in range(n_chip):
            jj = s * n_row + 2 * x + half
            far = far + multiply(b_all[2 * x + 1 - half, s], y_all[jj])
    far_part[...] = far
    to_diag = pltpu.make_async_remote_copy(
        far_part, got_diag, p_send.at[0], p_recv.at[0],
        device_id=diagonal, device_id_type=MESH)
    to_plane = pltpu.make_async_remote_copy(
        far_part, got_plane, p_send.at[1], p_recv.at[1],
        device_id=plane_peer, device_id_type=MESH)
    to_diag.start()
    to_plane.start()
    own = jnp.zeros(own_part.shape, jnp.float32)
    for s in range(slots):
        for x in range(n_chip):
            jj = s * n_row + 2 * x + half
            own = own + multiply(b_all[2 * x + half, s], y_all[jj])
    own_part[...] = own
    to_layer = pltpu.make_async_remote_copy(
        own_part, got_layer, p_send.at[2], p_recv.at[2],
        device_id=layer_peer, device_id_type=MESH)
    to_layer.start()
    to_plane.wait()
    mine = own_part[...] + got_plane[...]
    to_diag.wait()
    to_layer.wait()
    o_ref[...] = a_ref[...] - (mine + (got_layer[...] + got_diag[...]))

    for copy in sends + b_sends:
        copy.wait_send()

    @pl.when(jnp.logical_not(keeper))
    def _():
        cross_fill.wait_send()


def shards(interface_panel, coupling, solved_coupling):
    n_row = lax.axis_size("row")
    n_col = lax.axis_size("col")
    _, slots, depth, width = coupling.shape
    vmem = pl.BlockSpec(memory_space=pltpu.VMEM)
    rows, cols = interface_panel.shape
    part = pltpu.VMEM((rows, cols), jnp.float32)
    return pl.pallas_call(
        kernel,
        out_shape=jax.ShapeDtypeStruct((rows, cols), jnp.float32),
        in_specs=[vmem, vmem, vmem],
        out_specs=vmem,
        scratch_shapes=[
            pltpu.VMEM((n_row, slots, depth, width), jnp.float32),
            pltpu.VMEM((n_col,) + solved_coupling.shape, jnp.float32),
            part, part, part, part, part,
            pltpu.SemaphoreType.DMA((n_row + 1,)),
            pltpu.SemaphoreType.DMA((n_row,)),
            pltpu.SemaphoreType.DMA((n_col,)),
            pltpu.SemaphoreType.DMA((n_col,)),
            pltpu.SemaphoreType.DMA((3,)),
            pltpu.SemaphoreType.DMA((3,)),
        ],
        compiler_params=pltpu.CompilerParams(collective_id=0, has_side_effects=True),
    )(interface_panel, coupling, solved_coupling)


def solution(mesh):
    return jax.shard_map(
        shards,
        mesh=mesh,
        in_specs=(P("col", "row"), P("layer", None, "row", "col"), P(("layer", "col"), "row")),
        out_specs=P("col", "row"),
        check_vma=False,
    )
```

```python
import jax
import jax.numpy as jnp
from jax import lax
from jax.experimental import pallas as pl
from jax.experimental.pallas import tpu as pltpu
from jax.sharding import PartitionSpec as P

MESH = pl.DeviceIdType.MESH
CHUNKS = 4


def multiply(block, solved):
    return lax.dot_general(
        block,
        solved,
        (((0,), (0,)), ((), ())),
        precision=lax.Precision.HIGHEST,
        preferred_element_type=jnp.float32,
    )


def kernel(b_ref, y_ref, o_ref, b_all, y_all, own_part, far_part, got_diag, got_plane, got_layer,
           b_send, b_recv, y_send, y_recv, p_send, p_recv):
    n_row = lax.axis_size("row")
    n_col = lax.axis_size("col")
    n_chip = n_row // 2
    n_z = n_col // 2
    slots = b_ref.shape[1]
    r = lax.axis_index("row")
    c = lax.axis_index("col")
    l = lax.axis_index("layer")
    chip, core = r // 2, r % 2
    z, half = c // 2, c % 2
    keeper = core == half

    def col_of(zz, h):
        return ((zz + n_z) % n_z) * 2 + h

    cw = col_of(z + 1, half)
    ccw = col_of(z - 1, half)
    partner_col = col_of(z, 1 - half)
    on_chip = chip * 2 + (1 - core)

    def far_row(d):
        return ((chip + d) % n_chip) * 2 + core

    cross = (on_chip, partner_col, l)
    diagonal = (r, partner_col, 1 - l)
    plane_peer = (r, partner_col, l)
    layer_peer = (r, c, 1 - l)

    barrier = pltpu.get_barrier_semaphore()
    peers = [(far_row(d), c, l) for d in range(1, n_chip)]
    peers += [(on_chip, c, l), cross, (r, cw, l), (r, ccw, l), diagonal, plane_peer, layer_peer]
    for peer in peers:
        pl.semaphore_signal(barrier, 1, device_id=peer, device_id_type=MESH)
    pl.semaphore_wait(barrier, len(peers))

    def arrival(src, dst, recv_sems, slot):
        pltpu.make_async_remote_copy(
            src, dst.at[slot], recv_sems.at[slot], recv_sems.at[slot],
            device_id=layer_peer, device_id_type=MESH).wait_recv()

    local_fill = pltpu.make_async_copy(b_ref.at[0], b_all.at[r], b_recv.at[r])
    cross_fill = pltpu.make_async_remote_copy(
        b_ref.at[0], b_all.at[on_chip], b_send.at[0], b_recv.at[on_chip],
        device_id=cross, device_id_type=MESH)

    @pl.when(keeper)
    def _():
        local_fill.start()

    @pl.when(jnp.logical_not(keeper))
    def _():
        cross_fill.start()

    sends = []
    rows_q = y_ref.shape[0] // CHUNKS

    def piece(q):
        return pl.ds(q * rows_q, rows_q)

    def y_send_chunk(src, slot, q, col):
        copy = pltpu.make_async_remote_copy(
            src.at[piece(q)], y_all.at[slot, piece(q)], y_send.at[len(sends)], y_recv.at[slot, q],
            device_id=(r, col, l), device_id_type=MESH)
        copy.start()
        sends.append(copy)

    def y_arrival(slot, q):
        pltpu.make_async_remote_copy(
            y_ref.at[piece(q)], y_all.at[slot, piece(q)], y_recv.at[slot, q], y_recv.at[slot, q],
            device_id=layer_peer, device_id_type=MESH).wait_recv()

    steps = n_z // 2
    low, high = list(range(CHUNKS // 2)), list(range(CHUNKS // 2, CHUNKS))

    def cw_chunks(t):
        return list(range(CHUNKS)) if t < steps else low

    def ccw_chunks(t):
        return list(range(CHUNKS)) if t < steps else high

    for q in cw_chunks(1):
        y_send_chunk(y_ref, c, q, cw)
    for q in ccw_chunks(1):
        y_send_chunk(y_ref, c, q, ccw)
    y_all[c] = y_ref[...]

    @pl.when(keeper)
    def _():
        local_fill.wait()

    @pl.when(jnp.logical_not(keeper))
    def _():
        arrival(b_ref.at[0], b_all, b_recv, r)

    b_sends = []

    def b_send_slot(slot, row):
        copy = pltpu.make_async_remote_copy(
            b_all.at[slot], b_all.at[slot], b_send.at[1 + len(b_sends)], b_recv.at[slot],
            device_id=(row, c, l), device_id_type=MESH)
        copy.start()
        b_sends.append(copy)

    for d in range(1, n_chip):
        b_send_slot(r, far_row(d))
    b_send_slot(r, on_chip)

    for t in range(2, steps + 1):
        for q in range(CHUNKS):
            if q in cw_chunks(t - 1):
                slot = col_of(z - (t - 1), half)
                y_arrival(slot, q)
                if q in cw_chunks(t):
                    y_send_chunk(y_all.at[slot], slot, q, cw)
            if q in ccw_chunks(t - 1):
                slot = col_of(z + (t - 1), half)
                y_arrival(slot, q)
                if q in ccw_chunks(t):
                    y_send_chunk(y_all.at[slot], slot, q, ccw)

    for d in range(1, n_chip):
        slot = far_row(d)
        arrival(b_ref.at[0], b_all, b_recv, slot)
        b_send_slot(slot, on_chip)

    for q in range(CHUNKS):
        y_arrival(col_of(z - steps, half), q)
    arrival(b_ref.at[0], b_all, b_recv, on_chip)
    for d in range(1, n_chip):
        arrival(b_ref.at[0], b_all, b_recv, ((chip + d) % n_chip) * 2 + (1 - core))

    far = jnp.zeros(far_part.shape, jnp.float32)
    for s in range(slots):
        for x in range(n_chip):
            jj = s * n_row + 2 * x + half
            far = far + multiply(b_all[2 * x + 1 - half, s], y_all[jj])
    far_part[...] = far
    to_diag = pltpu.make_async_remote_copy(
        far_part, got_diag, p_send.at[0], p_recv.at[0],
        device_id=diagonal, device_id_type=MESH)
    to_plane = pltpu.make_async_remote_copy(
        far_part, got_plane, p_send.at[1], p_recv.at[1],
        device_id=plane_peer, device_id_type=MESH)
    to_diag.start()
    to_plane.start()
    own = jnp.zeros(own_part.shape, jnp.float32)
    for s in range(slots):
        for x in range(n_chip):
            jj = s * n_row + 2 * x + half
            own = own + multiply(b_all[2 * x + half, s], y_all[jj])
    own_part[...] = own
    to_layer = pltpu.make_async_remote_copy(
        own_part, got_layer, p_send.at[2], p_recv.at[2],
        device_id=layer_peer, device_id_type=MESH)
    to_layer.start()
    to_plane.wait()
    mine = own_part[...] + got_plane[...]
    to_diag.wait()
    to_layer.wait()
    o_ref[...] = mine + (got_layer[...] + got_diag[...])

    for copy in sends + b_sends:
        copy.wait_send()

    @pl.when(jnp.logical_not(keeper))
    def _():
        cross_fill.wait_send()


def shards(interface_panel, coupling, solved_coupling):
    n_row = lax.axis_size("row")
    n_col = lax.axis_size("col")
    _, slots, depth, width = coupling.shape
    vmem = pl.BlockSpec(memory_space=pltpu.VMEM)
    rows, cols = interface_panel.shape
    part = pltpu.VMEM((rows, cols), jnp.float32)
    summed = pl.pallas_call(
        kernel,
        out_shape=jax.ShapeDtypeStruct((rows, cols), jnp.float32),
        in_specs=[vmem, vmem],
        out_specs=vmem,
        scratch_shapes=[
            pltpu.VMEM((n_row, slots, depth, width), jnp.float32),
            pltpu.VMEM((n_col,) + solved_coupling.shape, jnp.float32),
            part, part, part, part, part,
            pltpu.SemaphoreType.DMA((n_row + 1,)),
            pltpu.SemaphoreType.DMA((n_row,)),
            pltpu.SemaphoreType.DMA((n_col * CHUNKS,)),
            pltpu.SemaphoreType.DMA((n_col, CHUNKS)),
            pltpu.SemaphoreType.DMA((3,)),
            pltpu.SemaphoreType.DMA((3,)),
        ],
        compiler_params=pltpu.CompilerParams(collective_id=0, has_side_effects=True),
    )(coupling, solved_coupling)
    return interface_panel - summed


def solution(mesh):
    return jax.shard_map(
        shards,
        mesh=mesh,
        in_specs=(P("col", "row"), P("layer", None, "row", "col"), P(("layer", "col"), "row")),
        out_specs=P("col", "row"),
        check_vma=False,
    )
```

```python
import jax
import jax.numpy as jnp
from jax import lax
from jax.experimental import pallas as pl
from jax.experimental.pallas import tpu as pltpu
from jax.sharding import PartitionSpec as P

MESH = pl.DeviceIdType.MESH
CHUNKS = 4


def multiply(block, solved):
    return lax.dot_general(
        block,
        solved,
        (((0,), (0,)), ((), ())),
        precision=lax.Precision.HIGH,
        preferred_element_type=jnp.float32,
    )


def kernel(b_ref, y_ref, o_ref, b_all, y_all, own_part, far_part, got_diag, got_plane, got_layer,
           b_send, b_recv, y_send, y_recv, p_send, p_recv):
    n_row = lax.axis_size("row")
    n_col = lax.axis_size("col")
    n_chip = n_row // 2
    n_z = n_col // 2
    slots = b_ref.shape[1]
    r = lax.axis_index("row")
    c = lax.axis_index("col")
    l = lax.axis_index("layer")
    chip, core = r // 2, r % 2
    z, half = c // 2, c % 2
    keeper = core == half

    def col_of(zz, h):
        return ((zz + n_z) % n_z) * 2 + h

    cw = col_of(z + 1, half)
    ccw = col_of(z - 1, half)
    partner_col = col_of(z, 1 - half)
    on_chip = chip * 2 + (1 - core)

    def far_row(d):
        return ((chip + d) % n_chip) * 2 + core

    cross = (on_chip, partner_col, l)
    diagonal = (r, partner_col, 1 - l)
    plane_peer = (r, partner_col, l)
    layer_peer = (r, c, 1 - l)

    barrier = pltpu.get_barrier_semaphore()
    peers = [(far_row(d), c, l) for d in range(1, n_chip)]
    peers += [(on_chip, c, l), cross, (r, cw, l), (r, ccw, l), diagonal, plane_peer, layer_peer]
    for peer in peers:
        pl.semaphore_signal(barrier, 1, device_id=peer, device_id_type=MESH)
    pl.semaphore_wait(barrier, len(peers))

    def arrival(src, dst, recv_sems, slot):
        pltpu.make_async_remote_copy(
            src, dst.at[slot], recv_sems.at[slot], recv_sems.at[slot],
            device_id=layer_peer, device_id_type=MESH).wait_recv()

    local_fill = pltpu.make_async_copy(b_ref.at[0], b_all.at[r], b_recv.at[r])
    cross_fill = pltpu.make_async_remote_copy(
        b_ref.at[0], b_all.at[on_chip], b_send.at[0], b_recv.at[on_chip],
        device_id=cross, device_id_type=MESH)

    @pl.when(keeper)
    def _():
        local_fill.start()

    @pl.when(jnp.logical_not(keeper))
    def _():
        cross_fill.start()

    sends = []
    rows_q = y_ref.shape[0] // CHUNKS

    def piece(q):
        return pl.ds(q * rows_q, rows_q)

    def y_send_chunk(src, slot, q, col):
        copy = pltpu.make_async_remote_copy(
            src.at[piece(q)], y_all.at[slot, piece(q)], y_send.at[len(sends)], y_recv.at[slot, q],
            device_id=(r, col, l), device_id_type=MESH)
        copy.start()
        sends.append(copy)

    def y_arrival(slot, q):
        pltpu.make_async_remote_copy(
            y_ref.at[piece(q)], y_all.at[slot, piece(q)], y_recv.at[slot, q], y_recv.at[slot, q],
            device_id=layer_peer, device_id_type=MESH).wait_recv()

    steps = n_z // 2
    low, high = list(range(CHUNKS // 2)), list(range(CHUNKS // 2, CHUNKS))

    def cw_chunks(t):
        return list(range(CHUNKS)) if t < steps else low

    def ccw_chunks(t):
        return list(range(CHUNKS)) if t < steps else high

    for q in cw_chunks(1):
        y_send_chunk(y_ref, c, q, cw)
    for q in ccw_chunks(1):
        y_send_chunk(y_ref, c, q, ccw)
    y_all[c] = y_ref[...]

    @pl.when(keeper)
    def _():
        local_fill.wait()

    @pl.when(jnp.logical_not(keeper))
    def _():
        arrival(b_ref.at[0], b_all, b_recv, r)

    b_sends = []

    def b_send_slot(slot, row):
        copy = pltpu.make_async_remote_copy(
            b_all.at[slot], b_all.at[slot], b_send.at[1 + len(b_sends)], b_recv.at[slot],
            device_id=(row, c, l), device_id_type=MESH)
        copy.start()
        b_sends.append(copy)

    for d in range(1, n_chip):
        b_send_slot(r, far_row(d))
    b_send_slot(r, on_chip)

    for t in range(2, steps + 1):
        for q in range(CHUNKS):
            if q in cw_chunks(t - 1):
                slot = col_of(z - (t - 1), half)
                y_arrival(slot, q)
                if q in cw_chunks(t):
                    y_send_chunk(y_all.at[slot], slot, q, cw)
            if q in ccw_chunks(t - 1):
                slot = col_of(z + (t - 1), half)
                y_arrival(slot, q)
                if q in ccw_chunks(t):
                    y_send_chunk(y_all.at[slot], slot, q, ccw)

    for d in range(1, n_chip):
        slot = far_row(d)
        arrival(b_ref.at[0], b_all, b_recv, slot)
        b_send_slot(slot, on_chip)

    for q in range(CHUNKS):
        y_arrival(col_of(z - steps, half), q)
    arrival(b_ref.at[0], b_all, b_recv, on_chip)
    for d in range(1, n_chip):
        arrival(b_ref.at[0], b_all, b_recv, ((chip + d) % n_chip) * 2 + (1 - core))

    far = jnp.zeros(far_part.shape, jnp.float32)
    for s in range(slots):
        for x in range(n_chip):
            jj = s * n_row + 2 * x + half
            far = far + multiply(b_all[2 * x + 1 - half, s], y_all[jj])
    far_part[...] = far
    to_diag = pltpu.make_async_remote_copy(
        far_part, got_diag, p_send.at[0], p_recv.at[0],
        device_id=diagonal, device_id_type=MESH)
    to_plane = pltpu.make_async_remote_copy(
        far_part, got_plane, p_send.at[1], p_recv.at[1],
        device_id=plane_peer, device_id_type=MESH)
    to_diag.start()
    to_plane.start()
    own = jnp.zeros(own_part.shape, jnp.float32)
    for s in range(slots):
        for x in range(n_chip):
            jj = s * n_row + 2 * x + half
            own = own + multiply(b_all[2 * x + half, s], y_all[jj])
    own_part[...] = own
    to_layer = pltpu.make_async_remote_copy(
        own_part, got_layer, p_send.at[2], p_recv.at[2],
        device_id=layer_peer, device_id_type=MESH)
    to_layer.start()
    to_plane.wait()
    mine = own_part[...] + got_plane[...]
    to_diag.wait()
    to_layer.wait()
    o_ref[...] = mine + (got_layer[...] + got_diag[...])

    for copy in sends + b_sends:
        copy.wait_send()

    @pl.when(jnp.logical_not(keeper))
    def _():
        cross_fill.wait_send()


def shards(interface_panel, coupling, solved_coupling):
    n_row = lax.axis_size("row")
    n_col = lax.axis_size("col")
    _, slots, depth, width = coupling.shape
    vmem = pl.BlockSpec(memory_space=pltpu.VMEM)
    rows, cols = interface_panel.shape
    part = pltpu.VMEM((rows, cols), jnp.float32)
    summed = pl.pallas_call(
        kernel,
        out_shape=jax.ShapeDtypeStruct((rows, cols), jnp.float32),
        in_specs=[vmem, vmem],
        out_specs=vmem,
        scratch_shapes=[
            pltpu.VMEM((n_row, slots, depth, width), jnp.float32),
            pltpu.VMEM((n_col,) + solved_coupling.shape, jnp.float32),
            part, part, part, part, part,
            pltpu.SemaphoreType.DMA((n_row + 1,)),
            pltpu.SemaphoreType.DMA((n_row,)),
            pltpu.SemaphoreType.DMA((n_col * CHUNKS,)),
            pltpu.SemaphoreType.DMA((n_col, CHUNKS)),
            pltpu.SemaphoreType.DMA((3,)),
            pltpu.SemaphoreType.DMA((3,)),
        ],
        compiler_params=pltpu.CompilerParams(collective_id=0, has_side_effects=True),
    )(coupling, solved_coupling)
    return interface_panel - summed


def solution(mesh):
    return jax.shard_map(
        shards,
        mesh=mesh,
        in_specs=(P("col", "row"), P("layer", None, "row", "col"), P(("layer", "col"), "row")),
        out_specs=P("col", "row"),
        check_vma=False,
    )
```

```python
import jax
import jax.numpy as jnp
from jax import lax
from jax.experimental import pallas as pl
from jax.experimental.pallas import tpu as pltpu
from jax.sharding import PartitionSpec as P

MESH = pl.DeviceIdType.MESH
CHUNKS = 4


def multiply(block, solved):
    return lax.dot_general(
        block,
        solved,
        (((0,), (0,)), ((), ())),
        precision=lax.Precision.HIGHEST,
        preferred_element_type=jnp.float32,
    )


def kernel(b_ref, y_ref, o_ref, b_all, y_all, own_part, far_part, got_diag, got_plane, got_layer,
           b_send, b_recv, y_send, y_recv, p_send, p_recv):
    n_row = lax.axis_size("row")
    n_col = lax.axis_size("col")
    n_chip = n_row // 2
    n_z = n_col // 2
    slots = b_ref.shape[1]
    r = lax.axis_index("row")
    c = lax.axis_index("col")
    l = lax.axis_index("layer")
    chip, core = r // 2, r % 2
    z, half = c // 2, c % 2
    keeper = core == half

    def col_of(zz, h):
        return ((zz + n_z) % n_z) * 2 + h

    cw = col_of(z + 1, half)
    ccw = col_of(z - 1, half)
    partner_col = col_of(z, 1 - half)
    on_chip = chip * 2 + (1 - core)

    def far_row(d):
        return ((chip + d) % n_chip) * 2 + core

    cross = (on_chip, partner_col, l)
    diagonal = (r, partner_col, 1 - l)
    plane_peer = (r, partner_col, l)
    layer_peer = (r, c, 1 - l)

    barrier = pltpu.get_barrier_semaphore()
    peers = [(far_row(d), c, l) for d in range(1, n_chip)]
    peers += [(on_chip, c, l), cross, (r, cw, l), (r, ccw, l), diagonal, plane_peer, layer_peer]
    for peer in peers:
        pl.semaphore_signal(barrier, 1, device_id=peer, device_id_type=MESH)
    pl.semaphore_wait(barrier, len(peers))

    def arrival(src, dst, recv_sems, slot):
        pltpu.make_async_remote_copy(
            src, dst.at[slot], recv_sems.at[slot], recv_sems.at[slot],
            device_id=layer_peer, device_id_type=MESH).wait_recv()

    rows_b = b_ref.shape[2] // CHUNKS

    def bpiece(q):
        return pl.ds(q * rows_b, rows_b)

    local_fill = [pltpu.make_async_copy(b_ref.at[0, :, bpiece(q)], b_all.at[r, :, bpiece(q)], b_recv.at[r, q])
                  for q in range(CHUNKS)]
    cross_fill = [pltpu.make_async_remote_copy(
        b_ref.at[0, :, bpiece(q)], b_all.at[on_chip, :, bpiece(q)], b_send.at[q], b_recv.at[on_chip, q],
        device_id=cross, device_id_type=MESH) for q in range(CHUNKS)]

    @pl.when(keeper)
    def _():
        for copy in local_fill:
            copy.start()

    @pl.when(jnp.logical_not(keeper))
    def _():
        for copy in cross_fill:
            copy.start()

    sends = []
    rows_q = y_ref.shape[0] // CHUNKS

    def piece(q):
        return pl.ds(q * rows_q, rows_q)

    def y_send_chunk(src, slot, q, col):
        copy = pltpu.make_async_remote_copy(
            src.at[piece(q)], y_all.at[slot, piece(q)], y_send.at[len(sends)], y_recv.at[slot, q],
            device_id=(r, col, l), device_id_type=MESH)
        copy.start()
        sends.append(copy)

    def y_arrival(slot, q):
        pltpu.make_async_remote_copy(
            y_ref.at[piece(q)], y_all.at[slot, piece(q)], y_recv.at[slot, q], y_recv.at[slot, q],
            device_id=layer_peer, device_id_type=MESH).wait_recv()

    def b_arrival(slot, q):
        pltpu.make_async_remote_copy(
            b_ref.at[0, :, bpiece(q)], b_all.at[slot, :, bpiece(q)], b_recv.at[slot, q], b_recv.at[slot, q],
            device_id=layer_peer, device_id_type=MESH).wait_recv()

    steps = n_z // 2
    low, high = list(range(CHUNKS // 2)), list(range(CHUNKS // 2, CHUNKS))

    def cw_chunks(t):
        return list(range(CHUNKS)) if t < steps else low

    def ccw_chunks(t):
        return list(range(CHUNKS)) if t < steps else high

    for q in cw_chunks(1):
        y_send_chunk(y_ref, c, q, cw)
    for q in ccw_chunks(1):
        y_send_chunk(y_ref, c, q, ccw)
    y_all[c] = y_ref[...]

    b_sends = []

    def b_send_chunk(slot, q, row):
        copy = pltpu.make_async_remote_copy(
            b_all.at[slot, :, bpiece(q)], b_all.at[slot, :, bpiece(q)], b_send.at[CHUNKS + len(b_sends)],
            b_recv.at[slot, q], device_id=(row, c, l), device_id_type=MESH)
        copy.start()
        b_sends.append(copy)

    def b_broadcast():
        for q in range(CHUNKS):
            @pl.when(keeper)
            def _():
                local_fill[q].wait()

            @pl.when(jnp.logical_not(keeper))
            def _():
                b_arrival(r, q)

            for d in range(1, n_chip):
                b_send_chunk(r, q, far_row(d))
            b_send_chunk(r, q, on_chip)

    def b_relay():
        for d in range(1, n_chip):
            for q in range(CHUNKS):
                b_arrival(far_row(d), q)
                b_send_chunk(far_row(d), q, on_chip)

    def y_step(t):
        for q in range(CHUNKS):
            if q in cw_chunks(t - 1):
                slot = col_of(z - (t - 1), half)
                y_arrival(slot, q)
                if q in cw_chunks(t):
                    y_send_chunk(y_all.at[slot], slot, q, cw)
            if q in ccw_chunks(t - 1):
                slot = col_of(z + (t - 1), half)
                y_arrival(slot, q)
                if q in ccw_chunks(t):
                    y_send_chunk(y_all.at[slot], slot, q, ccw)

    pending = [b_broadcast, b_relay]
    for t in range(2, steps + 1):
        y_step(t)
        if pending:
            pending.pop(0)()
    for step in pending:
        step()

    for q in range(CHUNKS):
        y_arrival(col_of(z - steps, half), q)
    for q in range(CHUNKS):
        b_arrival(on_chip, q)
    for d in range(1, n_chip):
        for q in range(CHUNKS):
            b_arrival(((chip + d) % n_chip) * 2 + (1 - core), q)

    far = jnp.zeros(far_part.shape, jnp.float32)
    for s in range(slots):
        for x in range(n_chip):
            jj = s * n_row + 2 * x + half
            far = far + multiply(b_all[2 * x + 1 - half, s], y_all[jj])
    far_part[...] = far
    to_diag = pltpu.make_async_remote_copy(
        far_part, got_diag, p_send.at[0], p_recv.at[0],
        device_id=diagonal, device_id_type=MESH)
    to_plane = pltpu.make_async_remote_copy(
        far_part, got_plane, p_send.at[1], p_recv.at[1],
        device_id=plane_peer, device_id_type=MESH)
    to_diag.start()
    to_plane.start()
    own = jnp.zeros(own_part.shape, jnp.float32)
    for s in range(slots):
        for x in range(n_chip):
            jj = s * n_row + 2 * x + half
            own = own + multiply(b_all[2 * x + half, s], y_all[jj])
    own_part[...] = own
    to_layer = pltpu.make_async_remote_copy(
        own_part, got_layer, p_send.at[2], p_recv.at[2],
        device_id=layer_peer, device_id_type=MESH)
    to_layer.start()
    to_plane.wait()
    mine = own_part[...] + got_plane[...]
    to_diag.wait()
    to_layer.wait()
    o_ref[...] = mine + (got_layer[...] + got_diag[...])

    for copy in sends + b_sends:
        copy.wait_send()

    @pl.when(jnp.logical_not(keeper))
    def _():
        for copy in cross_fill:
            copy.wait_send()


def shards(interface_panel, coupling, solved_coupling):
    n_row = lax.axis_size("row")
    n_col = lax.axis_size("col")
    _, slots, depth, width = coupling.shape
    vmem = pl.BlockSpec(memory_space=pltpu.VMEM)
    rows, cols = interface_panel.shape
    part = pltpu.VMEM((rows, cols), jnp.float32)
    summed = pl.pallas_call(
        kernel,
        out_shape=jax.ShapeDtypeStruct((rows, cols), jnp.float32),
        in_specs=[vmem, vmem],
        out_specs=vmem,
        scratch_shapes=[
            pltpu.VMEM((n_row, slots, depth, width), jnp.float32),
            pltpu.VMEM((n_col,) + solved_coupling.shape, jnp.float32),
            part, part, part, part, part,
            pltpu.SemaphoreType.DMA((2 * n_row * CHUNKS,)),
            pltpu.SemaphoreType.DMA((n_row, CHUNKS)),
            pltpu.SemaphoreType.DMA((n_col * CHUNKS,)),
            pltpu.SemaphoreType.DMA((n_col, CHUNKS)),
            pltpu.SemaphoreType.DMA((3,)),
            pltpu.SemaphoreType.DMA((3,)),
        ],
        compiler_params=pltpu.CompilerParams(collective_id=0, has_side_effects=True),
    )(coupling, solved_coupling)
    return interface_panel - summed


def solution(mesh):
    return jax.shard_map(
        shards,
        mesh=mesh,
        in_specs=(P("col", "row"), P("layer", None, "row", "col"), P(("layer", "col"), "row")),
        out_specs=P("col", "row"),
        check_vma=False,
    )
```

```python
import jax
import jax.numpy as jnp
from jax import lax
from jax.experimental import pallas as pl
from jax.experimental.pallas import tpu as pltpu
from jax.sharding import PartitionSpec as P

MESH = pl.DeviceIdType.MESH
CHUNKS = 4


def multiply(block, solved):
    return lax.dot_general(
        block,
        solved,
        (((0,), (0,)), ((), ())),
        precision=lax.Precision.HIGHEST,
        preferred_element_type=jnp.float32,
    )


def kernel(b_ref, y_ref, o_ref, b_all, y_all, own_part, far_part, got_diag, got_plane, got_layer,
           b_send, b_recv, y_send, y_recv, p_send, p_recv):
    n_row = lax.axis_size("row")
    n_col = lax.axis_size("col")
    n_chip = n_row // 2
    n_z = n_col // 2
    slots = b_ref.shape[1]
    r = lax.axis_index("row")
    c = lax.axis_index("col")
    l = lax.axis_index("layer")
    chip, core = r // 2, r % 2
    z, half = c // 2, c % 2
    keeper = core == half

    def col_of(zz, h):
        return ((zz + n_z) % n_z) * 2 + h

    cw = col_of(z + 1, half)
    ccw = col_of(z - 1, half)
    partner_col = col_of(z, 1 - half)
    on_chip = chip * 2 + (1 - core)

    def far_row(d):
        return ((chip + d) % n_chip) * 2 + core

    cross = (on_chip, partner_col, l)
    diagonal = (r, partner_col, 1 - l)
    plane_peer = (r, partner_col, l)
    layer_peer = (r, c, 1 - l)

    barrier = pltpu.get_barrier_semaphore()
    peers = [(far_row(d), c, l) for d in range(1, n_chip)]
    peers += [(on_chip, c, l), cross, (r, cw, l), (r, ccw, l), diagonal, plane_peer, layer_peer]
    for peer in peers:
        pl.semaphore_signal(barrier, 1, device_id=peer, device_id_type=MESH)
    pl.semaphore_wait(barrier, len(peers))

    def arrival(src, dst, recv_sems, slot):
        pltpu.make_async_remote_copy(
            src, dst.at[slot], recv_sems.at[slot], recv_sems.at[slot],
            device_id=layer_peer, device_id_type=MESH).wait_recv()

    local_fill = pltpu.make_async_copy(b_ref.at[0], b_all.at[r], b_recv.at[r])
    cross_fill = pltpu.make_async_remote_copy(
        b_ref.at[0], b_all.at[on_chip], b_send.at[0], b_recv.at[on_chip],
        device_id=cross, device_id_type=MESH)

    @pl.when(keeper)
    def _():
        local_fill.start()

    @pl.when(jnp.logical_not(keeper))
    def _():
        cross_fill.start()

    sends = []
    rows_q = y_ref.shape[0] // CHUNKS

    def piece(q):
        return pl.ds(q * rows_q, rows_q)

    def y_send_chunk(src, slot, q, col):
        copy = pltpu.make_async_remote_copy(
            src.at[piece(q)], y_all.at[slot, piece(q)], y_send.at[len(sends)], y_recv.at[slot, q],
            device_id=(r, col, l), device_id_type=MESH)
        copy.start()
        sends.append(copy)

    def y_arrival(slot, q):
        pltpu.make_async_remote_copy(
            y_ref.at[piece(q)], y_all.at[slot, piece(q)], y_recv.at[slot, q], y_recv.at[slot, q],
            device_id=layer_peer, device_id_type=MESH).wait_recv()

    steps = n_z // 2
    low, high = list(range(CHUNKS // 2)), list(range(CHUNKS // 2, CHUNKS))

    def cw_chunks(t):
        return list(range(CHUNKS)) if t < steps else low

    def ccw_chunks(t):
        return list(range(CHUNKS)) if t < steps else high

    for q in cw_chunks(1):
        y_send_chunk(y_ref, c, q, cw)
    for q in ccw_chunks(1):
        y_send_chunk(y_ref, c, q, ccw)
    y_all[c] = y_ref[...]

    @pl.when(keeper)
    def _():
        local_fill.wait()

    @pl.when(jnp.logical_not(keeper))
    def _():
        arrival(b_ref.at[0], b_all, b_recv, r)

    b_sends = []

    def b_send_slot(slot, row):
        copy = pltpu.make_async_remote_copy(
            b_all.at[slot], b_all.at[slot], b_send.at[1 + len(b_sends)], b_recv.at[slot],
            device_id=(row, c, l), device_id_type=MESH)
        copy.start()
        b_sends.append(copy)

    for d in range(1, n_chip):
        b_send_slot(r, far_row(d))
    b_send_slot(r, on_chip)

    for t in range(2, steps + 1):
        for q in range(CHUNKS):
            if q in cw_chunks(t - 1):
                slot = col_of(z - (t - 1), half)
                y_arrival(slot, q)
                if q in cw_chunks(t):
                    y_send_chunk(y_all.at[slot], slot, q, cw)
            if q in ccw_chunks(t - 1):
                slot = col_of(z + (t - 1), half)
                y_arrival(slot, q)
                if q in ccw_chunks(t):
                    y_send_chunk(y_all.at[slot], slot, q, ccw)

    for d in range(1, n_chip):
        slot = far_row(d)
        arrival(b_ref.at[0], b_all, b_recv, slot)
        b_send_slot(slot, on_chip)

    for q in range(CHUNKS):
        y_arrival(col_of(z - steps, half), q)
    same = jnp.zeros(far_part.shape, jnp.float32)
    for s in range(slots):
        for x in range(n_chip):
            jj = s * n_row + 2 * x + half
            same = same + multiply(b_all[2 * x + core, s], y_all[jj])
    other = jnp.zeros(far_part.shape, jnp.float32)
    for d in range(n_chip):
        partner_chip = (chip + d) % n_chip
        slot = partner_chip * 2 + (1 - core)
        arrival(b_ref.at[0], b_all, b_recv, slot)
        for s in range(slots):
            other = other + multiply(b_all[slot, s], y_all[s * n_row + 2 * partner_chip + half])
    far_part[...] = jnp.where(keeper, other, same)
    own_part[...] = jnp.where(keeper, same, other)
    to_diag = pltpu.make_async_remote_copy(
        far_part, got_diag, p_send.at[0], p_recv.at[0],
        device_id=diagonal, device_id_type=MESH)
    to_plane = pltpu.make_async_remote_copy(
        far_part, got_plane, p_send.at[1], p_recv.at[1],
        device_id=plane_peer, device_id_type=MESH)
    to_diag.start()
    to_plane.start()
    to_layer = pltpu.make_async_remote_copy(
        own_part, got_layer, p_send.at[2], p_recv.at[2],
        device_id=layer_peer, device_id_type=MESH)
    to_layer.start()
    to_plane.wait()
    mine = own_part[...] + got_plane[...]
    to_diag.wait()
    to_layer.wait()
    o_ref[...] = mine + (got_layer[...] + got_diag[...])

    for copy in sends + b_sends:
        copy.wait_send()

    @pl.when(jnp.logical_not(keeper))
    def _():
        cross_fill.wait_send()


def shards(interface_panel, coupling, solved_coupling):
    n_row = lax.axis_size("row")
    n_col = lax.axis_size("col")
    _, slots, depth, width = coupling.shape
    vmem = pl.BlockSpec(memory_space=pltpu.VMEM)
    rows, cols = interface_panel.shape
    part = pltpu.VMEM((rows, cols), jnp.float32)
    summed = pl.pallas_call(
        kernel,
        out_shape=jax.ShapeDtypeStruct((rows, cols), jnp.float32),
        in_specs=[vmem, vmem],
        out_specs=vmem,
        scratch_shapes=[
            pltpu.VMEM((n_row, slots, depth, width), jnp.float32),
            pltpu.VMEM((n_col,) + solved_coupling.shape, jnp.float32),
            part, part, part, part, part,
            pltpu.SemaphoreType.DMA((n_row + 1,)),
            pltpu.SemaphoreType.DMA((n_row,)),
            pltpu.SemaphoreType.DMA((n_col * CHUNKS,)),
            pltpu.SemaphoreType.DMA((n_col, CHUNKS)),
            pltpu.SemaphoreType.DMA((3,)),
            pltpu.SemaphoreType.DMA((3,)),
        ],
        compiler_params=pltpu.CompilerParams(collective_id=0, has_side_effects=True),
    )(coupling, solved_coupling)
    return interface_panel - summed


def solution(mesh):
    return jax.shard_map(
        shards,
        mesh=mesh,
        in_specs=(P("col", "row"), P("layer", None, "row", "col"), P(("layer", "col"), "row")),
        out_specs=P("col", "row"),
        check_vma=False,
    )
```

```python
import jax
import jax.numpy as jnp
from jax import lax
from jax.experimental import pallas as pl
from jax.experimental.pallas import tpu as pltpu
from jax.sharding import PartitionSpec as P

MESH = pl.DeviceIdType.MESH
CHUNKS = 4


def multiply(block, solved):
    return lax.dot_general(
        block,
        solved,
        (((0,), (0,)), ((), ())),
        precision=lax.Precision.HIGHEST,
        preferred_element_type=jnp.float32,
    )


def kernel(b_ref, y_ref, o_ref, b_all, y_all, own_part, far_part, got_diag, got_plane, got_layer,
           b_send, b_recv, y_send, y_recv, p_send, p_recv):
    n_row = lax.axis_size("row")
    n_col = lax.axis_size("col")
    n_chip = n_row // 2
    n_z = n_col // 2
    slots = b_ref.shape[1]
    r = lax.axis_index("row")
    c = lax.axis_index("col")
    l = lax.axis_index("layer")
    chip, core = r // 2, r % 2
    z, half = c // 2, c % 2
    keeper = core == half

    def col_of(zz, h):
        return ((zz + n_z) % n_z) * 2 + h

    cw = col_of(z + 1, half)
    ccw = col_of(z - 1, half)
    partner_col = col_of(z, 1 - half)
    on_chip = chip * 2 + (1 - core)

    def far_row(d):
        return ((chip + d) % n_chip) * 2 + core

    cross = (on_chip, partner_col, l)
    diagonal = (r, partner_col, 1 - l)
    plane_peer = (r, partner_col, l)
    layer_peer = (r, c, 1 - l)

    barrier = pltpu.get_barrier_semaphore()
    peers = [(far_row(d), c, l) for d in range(1, n_chip)]
    peers += [(on_chip, c, l), cross, (r, cw, l), (r, ccw, l), diagonal, plane_peer, layer_peer]
    for peer in peers:
        pl.semaphore_signal(barrier, 1, device_id=peer, device_id_type=MESH)
    pl.semaphore_wait(barrier, len(peers))

    def arrival(src, dst, recv_sems, slot):
        pltpu.make_async_remote_copy(
            src, dst.at[slot], recv_sems.at[slot], recv_sems.at[slot],
            device_id=layer_peer, device_id_type=MESH).wait_recv()

    local_fill = pltpu.make_async_copy(b_ref.at[0], b_all.at[r], b_recv.at[r])
    cross_fill = pltpu.make_async_remote_copy(
        b_ref.at[0], b_all.at[on_chip], b_send.at[0], b_recv.at[on_chip],
        device_id=cross, device_id_type=MESH)

    @pl.when(keeper)
    def _():
        local_fill.start()

    @pl.when(jnp.logical_not(keeper))
    def _():
        cross_fill.start()

    sends = []
    rows_q = y_ref.shape[0] // CHUNKS

    def piece(q):
        return pl.ds(q * rows_q, rows_q)

    def y_send_chunk(src, slot, q, col):
        copy = pltpu.make_async_remote_copy(
            src.at[piece(q)], y_all.at[slot, piece(q)], y_send.at[len(sends)], y_recv.at[slot, q],
            device_id=(r, col, l), device_id_type=MESH)
        copy.start()
        sends.append(copy)

    def y_arrival(slot, q):
        pltpu.make_async_remote_copy(
            y_ref.at[piece(q)], y_all.at[slot, piece(q)], y_recv.at[slot, q], y_recv.at[slot, q],
            device_id=layer_peer, device_id_type=MESH).wait_recv()

    steps = n_z // 2
    low, high = list(range(CHUNKS // 2)), list(range(CHUNKS // 2, CHUNKS))

    def cw_chunks(t):
        return list(range(CHUNKS)) if t < steps else low

    def ccw_chunks(t):
        return list(range(CHUNKS)) if t < steps else high

    for q in cw_chunks(1):
        y_send_chunk(y_ref, c, q, cw)
    for q in ccw_chunks(1):
        y_send_chunk(y_ref, c, q, ccw)
    y_all[c] = y_ref[...]

    @pl.when(keeper)
    def _():
        local_fill.wait()

    @pl.when(jnp.logical_not(keeper))
    def _():
        arrival(b_ref.at[0], b_all, b_recv, r)

    b_sends = []

    def b_send_slot(slot, row):
        copy = pltpu.make_async_remote_copy(
            b_all.at[slot], b_all.at[slot], b_send.at[1 + len(b_sends)], b_recv.at[slot],
            device_id=(row, c, l), device_id_type=MESH)
        copy.start()
        b_sends.append(copy)

    for d in range(1, n_chip):
        b_send_slot(r, far_row(d))
    b_send_slot(r, on_chip)

    for t in range(2, steps + 1):
        for q in range(CHUNKS):
            if q in cw_chunks(t - 1):
                slot = col_of(z - (t - 1), half)
                y_arrival(slot, q)
                if q in cw_chunks(t):
                    y_send_chunk(y_all.at[slot], slot, q, cw)
            if q in ccw_chunks(t - 1):
                slot = col_of(z + (t - 1), half)
                y_arrival(slot, q)
                if q in ccw_chunks(t):
                    y_send_chunk(y_all.at[slot], slot, q, ccw)

    for d in range(1, n_chip):
        slot = far_row(d)
        arrival(b_ref.at[0], b_all, b_recv, slot)
        b_send_slot(slot, on_chip)

    for q in range(CHUNKS):
        y_arrival(col_of(z - steps, half), q)
    far = jnp.zeros(far_part.shape, jnp.float32)
    for x in range(n_chip):
        slot = 2 * x + 1 - half

        @pl.when(keeper)
        def _():
            arrival(b_ref.at[0], b_all, b_recv, slot)

        for s in range(slots):
            far = far + multiply(b_all[slot, s], y_all[s * n_row + 2 * x + half])
    far_part[...] = far
    to_diag = pltpu.make_async_remote_copy(
        far_part, got_diag, p_send.at[0], p_recv.at[0],
        device_id=diagonal, device_id_type=MESH)
    to_plane = pltpu.make_async_remote_copy(
        far_part, got_plane, p_send.at[1], p_recv.at[1],
        device_id=plane_peer, device_id_type=MESH)
    to_diag.start()
    to_plane.start()
    own = jnp.zeros(own_part.shape, jnp.float32)
    for x in range(n_chip):
        slot = 2 * x + half

        @pl.when(jnp.logical_not(keeper))
        def _():
            arrival(b_ref.at[0], b_all, b_recv, slot)

        for s in range(slots):
            own = own + multiply(b_all[slot, s], y_all[s * n_row + 2 * x + half])
    own_part[...] = own
    to_layer = pltpu.make_async_remote_copy(
        own_part, got_layer, p_send.at[2], p_recv.at[2],
        device_id=layer_peer, device_id_type=MESH)
    to_layer.start()
    to_plane.wait()
    mine = own_part[...] + got_plane[...]
    to_diag.wait()
    to_layer.wait()
    o_ref[...] = mine + (got_layer[...] + got_diag[...])

    for copy in sends + b_sends:
        copy.wait_send()

    @pl.when(jnp.logical_not(keeper))
    def _():
        cross_fill.wait_send()


def shards(interface_panel, coupling, solved_coupling):
    n_row = lax.axis_size("row")
    n_col = lax.axis_size("col")
    _, slots, depth, width = coupling.shape
    vmem = pl.BlockSpec(memory_space=pltpu.VMEM)
    rows, cols = interface_panel.shape
    part = pltpu.VMEM((rows, cols), jnp.float32)
    summed = pl.pallas_call(
        kernel,
        out_shape=jax.ShapeDtypeStruct((rows, cols), jnp.float32),
        in_specs=[vmem, vmem],
        out_specs=vmem,
        scratch_shapes=[
            pltpu.VMEM((n_row, slots, depth, width), jnp.float32),
            pltpu.VMEM((n_col,) + solved_coupling.shape, jnp.float32),
            part, part, part, part, part,
            pltpu.SemaphoreType.DMA((n_row + 1,)),
            pltpu.SemaphoreType.DMA((n_row,)),
            pltpu.SemaphoreType.DMA((n_col * CHUNKS,)),
            pltpu.SemaphoreType.DMA((n_col, CHUNKS)),
            pltpu.SemaphoreType.DMA((3,)),
            pltpu.SemaphoreType.DMA((3,)),
        ],
        compiler_params=pltpu.CompilerParams(collective_id=0, has_side_effects=True),
    )(coupling, solved_coupling)
    return interface_panel - summed


def solution(mesh):
    return jax.shard_map(
        shards,
        mesh=mesh,
        in_specs=(P("col", "row"), P("layer", None, "row", "col"), P(("layer", "col"), "row")),
        out_specs=P("col", "row"),
        check_vma=False,
    )
```
